32 devices in a mesh: grp: 2 (over y), seq: 4 (over z), head: 2 (over x), sub: 2 (over core).
Axes of the slice: x: 2, y: 2, z: 4, core: 2. Of those that a mesh axis runs over, the one named last changes fastest.
Arguments:
- queries: bfloat16 [768, 5120], P(('grp', 'seq', 'head', 'sub')), parts along dimension 0, may hold values from -24 to 24
- keys: bfloat16 [768, 5120], P(('grp', 'seq', 'head', 'sub')), parts along dimension 0, may hold values from -24 to 24
- values: bfloat16 [768, 5120], P(('grp', 'seq', 'head', 'sub')), parts along dimension 0, may hold values from -6 to 6
- q_gain: float32 [5120], replicated, may hold values from 0.5 to 4
- k_gain: float32 [5120], replicated, may hold values from 0.5 to 4
Outputs:
- attended: bfloat16 [768, 5120], P(('grp', 'seq', 'head', 'sub')), parts along dimension 0
The draws below stay inside these ranges and needn't reach their ends.
There are 2 independent parts, one for each index of `grp`. The reference program is written for one: setup_inputs(seed, part) draws one part's arguments, and reference() takes and returns one part's arrays. A program takes and returns all parts, laid end to end along the dimension named above; an argument that names none is the same for every part. Nothing has to cross between parts.
All inputs are finite; a program needn't handle non-finite values.
Results may differ from the reference program's by a relative error of at most 0.012.
The reference program's roundings to bfloat16 on the way (of `q_normed`, `k_normed` and `probs`) count: a program that leaves them out, or rounds other values in their place, can miss the bound.
Values may be sent and summed in bfloat16 or wider, within the bound.
A program may use at most 64 MiB of HBM per device.

```python
import math
import jax
import jax.numpy as jnp
from jax import lax

H = 40
HD = 128
TOKENS = 384
WIDTH = 5120


def base_matrix(key, which):
    source = jax.random.fold_in(key, 40 + which)
    return jnp.clip(jax.random.normal(source, (TOKENS, H * HD), jnp.float32), -6.0, 6.0)


def draw_queries(key, part):
    matrix = base_matrix(key, 0)
    return matrix.astype(jnp.bfloat16)


def draw_keys(key, part):
    matrix = base_matrix(key, 1)
    return matrix.astype(jnp.bfloat16)


def block_scale(own_key, extent, shards, least, high):
    def one(dim, blocks):
        steps = jax.random.uniform(jax.random.fold_in(jax.random.fold_in(own_key, 6), dim), (blocks,), jnp.float32, least / len(shards), high / len(shards))
        return jnp.repeat(jnp.exp(steps), extent[dim] // blocks).reshape((-1,) + (1,) * (len(extent) - dim - 1))

    loudness = one(*shards[0])
    for cut in shards[1:]:
        loudness = loudness * one(*cut)
    return loudness


def gaussian(own_key, extent, spread, limit, shards=(), dtype=jnp.bfloat16):
    level = block_scale(own_key, extent, shards, -0.22, 0.18) if shards else 1.0
    values = jax.random.normal(own_key, extent, jnp.float32) * spread * level
    return jnp.minimum(jnp.maximum(values, -limit), limit).astype(dtype)


def setup_inputs(seed: int = 0, part: int = 0) -> dict:
    streams_of = jax.random.split(jax.random.key(seed), 6)
    part_splits = jax.random.split(jax.random.fold_in(streams_of[5], part), 6)
    queries = draw_queries(jax.random.fold_in(jax.random.fold_in(streams_of[5], part), 71), part)
    keys = draw_keys(jax.random.fold_in(jax.random.fold_in(streams_of[5], part), 71), part)
    values = gaussian(part_splits[2], (TOKENS, WIDTH), 1.0, 6.0, ((0, 16),))
    q_gain = jnp.clip(jnp.exp(jax.random.uniform(streams_of[3], (WIDTH,), jnp.float32, math.log(0.5), math.log(4.0))), 0.5, 4.0)
    k_gain = jnp.clip(jnp.exp(jax.random.uniform(streams_of[4], (WIDTH,), jnp.float32, math.log(0.5), math.log(4.0))), 0.5, 4.0)
    return {"queries": queries, "keys": keys, "values": values, "q_gain": q_gain, "k_gain": k_gain}


EPS = 1e-06

def normalize(matrix, gain):
    widened = matrix.astype(jnp.float32)
    inverse = lax.rsqrt(lax.optimization_barrier(jnp.mean(widened * widened, axis=-1, keepdims=True)) + EPS)
    return (widened * inverse * gain).astype(jnp.bfloat16)

def reference(queries, keys, values, q_gain, k_gain):
    q_normed = normalize(queries, q_gain)
    k_normed = normalize(keys, k_gain)
    q_heads = q_normed.reshape(TOKENS, H, HD).transpose(1, 0, 2)
    k_heads = k_normed.reshape(TOKENS, H, HD).transpose(1, 0, 2)
    v_heads = values.reshape(TOKENS, H, HD).transpose(1, 0, 2)
    block_size = math.gcd(TOKENS, 1024)
    factor = 1.0 / math.sqrt(HD)

    def one_head(triple):
        q_head, k_head, v_head = triple
        q_blocks = q_head.reshape(TOKENS // block_size, block_size, HD)

        def one_block(q_block):
            scores = jnp.dot(q_block, k_head.T, preferred_element_type=jnp.float32) * factor
            highest = lax.optimization_barrier(jnp.max(scores, axis=-1, keepdims=True))
            weights = jnp.exp(scores - highest)
            weight_sum = lax.optimization_barrier(jnp.sum(weights, axis=-1, keepdims=True))
            probs = weights.astype(jnp.bfloat16)
            weighted = jnp.dot(probs, v_head, preferred_element_type=jnp.float32)
            return (weighted / weight_sum).astype(jnp.bfloat16)
        return lax.map(one_block, q_blocks).reshape(TOKENS, HD)
    outputs = lax.map(one_head, (q_heads, k_heads, v_heads))
    return outputs.transpose(1, 0, 2).reshape(TOKENS, H * HD)
```

```python
import functools
import math

import jax
import jax.numpy as jnp
from jax import lax
from jax.experimental import pallas as pl
from jax.experimental.pallas import tpu as pltpu
from jax.sharding import PartitionSpec as P

HD = 128


EPS = 1e-06


def normalize(matrix, gain):
    widened = matrix.astype(jnp.float32)
    inverse = lax.rsqrt(jnp.mean(widened * widened, axis=-1, keepdims=True) + EPS)
    return (widened * inverse * gain).astype(jnp.bfloat16)


def body(queries, keys, values, q_gain, k_gain):
    q_normed = normalize(queries, q_gain)
    k_normed = normalize(keys, k_gain)
    q_local, k_local, v_local = (
        lax.all_to_all(q_normed, "head", split_axis=1, concat_axis=0, tiled=True),
        lax.all_to_all(k_normed, "head", split_axis=1, concat_axis=0, tiled=True),
        lax.all_to_all(values, "head", split_axis=1, concat_axis=0, tiled=True),
    )
    query_count = q_local.shape[0]
    local_heads = q_local.shape[1] // HD
    factor = 1.0 / math.sqrt(HD)
    q_heads = q_local.reshape(query_count, local_heads, HD).transpose(1, 0, 2)
    initial = (
        jnp.full((local_heads, query_count), -1e30, jnp.float32),
        jnp.zeros((local_heads, query_count), jnp.float32),
        jnp.zeros((local_heads, query_count, HD), jnp.float32),
    )
    half_rows = q_local.shape[0]
    key_piece = lax.all_gather(k_local, ("seq", "sub"), axis=0, tiled=True)
    value_piece = lax.all_gather(v_local, ("seq", "sub"), axis=0, tiled=True)
    row_count = key_piece.shape[0]
    block_size = math.gcd(row_count, 512)
    turn_count = row_count // block_size
    key_blocks = key_piece.reshape(turn_count, block_size, local_heads, HD)
    value_blocks = value_piece.reshape(turn_count, block_size, local_heads, HD)

    def advance(state, block_pair):
        key_block, value_block = block_pair
        highest, weight_sum, weighted = state
        scores = (
            jnp.einsum("hqd,khd->hqk", q_heads, key_block, preferred_element_type=jnp.float32)
            * factor
        )
        new_high = jnp.maximum(highest, jnp.max(scores, axis=-1))
        shrink = jnp.exp(highest - new_high)
        weights = jnp.exp(scores - new_high[..., None])
        new_sum = weight_sum * shrink + jnp.sum(weights, axis=-1)
        probs = weights.astype(jnp.bfloat16)
        added = jnp.einsum("hqk,khd->hqd", probs, value_block, preferred_element_type=jnp.float32)
        return ((new_high, new_sum, weighted * shrink[..., None] + added), None)

    partial_value = lax.scan(advance, initial, (key_blocks, value_blocks))[0]
    weight_sum = partial_value[1]
    weighted = partial_value[2]
    result = weighted / weight_sum[..., None]
    outputs = result.transpose(1, 0, 2).reshape(half_rows, local_heads * HD).astype(jnp.bfloat16)
    return lax.all_to_all(outputs, "head", split_axis=0, concat_axis=1, tiled=True)


MESH = pl.DeviceIdType.MESH


def kernel(sizes, rows, heads, q_hbm, k_hbm, v_hbm, qg_ref, kg_ref, out_ref,
           q_raw, k_raw, q_own, k_own, q_all, k_all, v_all, o_own,
           load_sem, local_sem, k_send, k_recv, v_send, v_recv, q_send, q_recv, o_send, o_recv):
    nz, nx, nc = sizes
    depth = nz // 2
    groups = depth * nx * nc
    count = heads // groups
    width = count * HD
    z, x, c = lax.axis_index("seq"), lax.axis_index("head"), lax.axis_index("sub")
    half, place = z // depth, z % depth
    mine = (place * nx + x) * nc + c

    def peer(dh, dp, dx, dc):
        tp, tx, tc = lax.rem(place + dp, depth), lax.rem(x + dx, nx), lax.rem(c + dc, nc)
        tz = lax.rem(half + dh, 2) * depth + tp
        return {"seq": tz, "head": tx, "sub": tc}, (tp * nx + tx) * nc + tc

    def back(dp, dx, dc):
        return peer(0, (depth - dp) % depth, (nx - dx) % nx, (nc - dc) % nc)[0]

    near = [(0, dp, dx, dc) for dp in range(depth) for dx in range(nx) for dc in range(nc)]
    far = [(1, dp, dx, dc) for dp in range(depth) for dx in range(nx) for dc in range(nc)]
    offsets = near + far

    loads = [
        pltpu.make_async_copy(q_hbm, q_raw, load_sem.at[0]),
        pltpu.make_async_copy(k_hbm, k_raw, load_sem.at[1]),
    ]
    for load in loads:
        load.start()

    barrier = pltpu.get_barrier_semaphore()
    for r in offsets[1:]:
        pl.semaphore_signal(barrier, inc=1, device_id=peer(*r)[0], device_id_type=MESH)

    def columns(group):
        return pl.ds(pl.multiple_of(group * width, HD), width)

    local_v = pltpu.make_async_copy(v_hbm.at[:, columns(mine)], v_all.at[0], local_sem.at[0])
    local_v.start()

    def norm(raw, gain, own):
        total = jnp.zeros((rows, HD), jnp.float32)
        for h in range(heads):
            block = raw[:, h * HD:(h + 1) * HD].astype(jnp.float32)
            total += block * block
        mean = jnp.sum(total, axis=-1, keepdims=True) / (heads * HD)
        inverse = lax.rsqrt(mean + EPS)
        for h in range(heads):
            block = raw[:, h * HD:(h + 1) * HD].astype(jnp.float32)
            j = h % count
            own[h // count, :, j * HD:(j + 1) * HD] = (
                block * inverse * gain[h:h + 1, :]
            ).astype(jnp.bfloat16)

    loads[1].wait()
    norm(k_raw, kg_ref, k_own)
    loads[0].wait()
    norm(q_raw, qg_ref, q_own)
    pl.semaphore_wait(barrier, len(offsets) - 1)

    order = far + near[1:]
    v_copies, k_copies, q_copies = {}, {}, {}
    for r in order:
        i = offsets.index(r)
        device, group = peer(*r)
        v_copies[i] = pltpu.make_async_remote_copy(
            v_hbm.at[:, columns(group)], v_all.at[i], v_send.at[i], v_recv.at[i],
            device_id=device, device_id_type=MESH)
        k_copies[i] = pltpu.make_async_remote_copy(
            k_own.at[group], k_all.at[i], k_send.at[i], k_recv.at[i],
            device_id=device, device_id_type=MESH)
        if r[0] == 0:
            q_copies[i] = pltpu.make_async_remote_copy(
                q_own.at[group], q_all.at[i], q_send.at[i], q_recv.at[i],
                device_id=device, device_id_type=MESH)
    for pair in zip(far, near):
        for r in pair:
            i = offsets.index(r)
            if i:
                k_copies[i].start()
                if i in q_copies:
                    q_copies[i].start()
                v_copies[i].start()

    local_k = pltpu.make_async_copy(k_own.at[mine], k_all.at[0], local_sem.at[1])
    local_q = pltpu.make_async_copy(q_own.at[mine], q_all.at[0], local_sem.at[2])
    local_k.start()
    local_q.start()
    local_k.wait()
    local_q.wait()
    local_v.wait()
    for copies in (q_copies, k_copies, v_copies):
        for i in sorted(copies):
            copies[i].wait_recv()

    factor = 1.0 / math.sqrt(HD)

    def stacked(ref, j):
        block = ref[:, :, j * HD:(j + 1) * HD].astype(jnp.float32)
        return block.reshape(ref.shape[0] * rows, HD).astype(jnp.bfloat16)

    for j in range(count):
        q, k, v = stacked(q_all, j), stacked(k_all, j), stacked(v_all, j)
        scores = lax.dot_general(
            q, k, (((1,), (1,)), ((), ())), preferred_element_type=jnp.float32) * factor
        weights = jnp.exp(scores - jnp.max(scores, axis=-1, keepdims=True))
        weight_sum = jnp.sum(weights, axis=-1, keepdims=True)
        weighted = jnp.dot(weights.astype(jnp.bfloat16), v, preferred_element_type=jnp.float32)
        result = (weighted / weight_sum).reshape(groups, rows, HD).astype(jnp.bfloat16)
        o_own[:, :, j * HD:(j + 1) * HD] = result

    o_copies = []
    for i, r in enumerate(near):
        if i:
            copy = pltpu.make_async_remote_copy(
                o_own.at[i], out_ref.at[:, columns(mine)], o_send.at[i], o_recv.at[i],
                device_id=back(*r[1:]), device_id_type=MESH)
            copy.start()
            o_copies.append(copy)
    local_o = pltpu.make_async_copy(o_own.at[0], out_ref.at[:, columns(mine)], local_sem.at[3])
    local_o.start()
    for copies in (k_copies, v_copies, q_copies):
        for i in sorted(copies):
            copies[i].wait_send()
    for copy in o_copies:
        copy.wait_send()
    for copy in o_copies:
        copy.wait_recv()
    local_o.wait()


def fused(sizes, queries, keys, values, q_gain, k_gain):
    rows, total_width = queries.shape
    heads = total_width // HD
    nz, nx, nc = sizes
    groups = nz // 2 * nx * nc
    width = heads // groups * HD
    everyone = groups * 2
    dma = pltpu.SemaphoreType.DMA
    half = jnp.bfloat16
    return pl.pallas_call(
        functools.partial(kernel, sizes, rows, heads),
        out_shape=jax.ShapeDtypeStruct((rows, total_width), half),
        in_specs=[pl.BlockSpec(memory_space=pl.ANY)] * 3
        + [pl.BlockSpec(memory_space=pltpu.VMEM)] * 2,
        out_specs=pl.BlockSpec(memory_space=pltpu.VMEM),
        scratch_shapes=[
            pltpu.VMEM((rows, total_width), half),
            pltpu.VMEM((rows, total_width), half),
            pltpu.VMEM((groups, rows, width), half),
            pltpu.VMEM((groups, rows, width), half),
            pltpu.VMEM((groups, rows, width), half),
            pltpu.VMEM((everyone, rows, width), half),
            pltpu.VMEM((everyone, rows, width), half),
            pltpu.VMEM((groups, rows, width), half),
            dma((2,)),
            dma((4,)),
            dma((everyone,)),
            dma((everyone,)),
            dma((everyone,)),
            dma((everyone,)),
            dma((groups,)),
            dma((groups,)),
            dma((groups,)),
            dma((groups,)),
        ],
        compiler_params=pltpu.CompilerParams(collective_id=0, has_side_effects=True),
    )(queries, keys, values, q_gain.reshape(heads, HD), k_gain.reshape(heads, HD))


def solution(mesh):
    spec = P(("grp", "seq", "head", "sub"), None)
    sizes = (mesh.shape["seq"], mesh.shape["head"], mesh.shape["sub"])

    def run(queries, keys, values, q_gain, k_gain):
        heads = queries.shape[1] // HD
        groups = sizes[0] // 2 * sizes[1] * sizes[2]
        fits = sizes[0] % 2 == 0 and groups <= 16 and heads % groups == 0
        if fits and queries.shape[0] % 8 == 0:
            return fused(sizes, queries, keys, values, q_gain, k_gain)
        return body(queries, keys, values, q_gain, k_gain)

    return jax.shard_map(
        run, mesh=mesh, in_specs=(spec, spec, spec, P(), P()), out_specs=spec, check_vma=False)
```

```python
import functools
import math

import jax
import jax.numpy as jnp
from jax import lax
from jax.experimental import pallas as pl
from jax.experimental.pallas import tpu as pltpu
from jax.sharding import PartitionSpec as P

HD = 128


EPS = 1e-06


def normalize(matrix, gain):
    widened = matrix.astype(jnp.float32)
    inverse = lax.rsqrt(jnp.mean(widened * widened, axis=-1, keepdims=True) + EPS)
    return (widened * inverse * gain).astype(jnp.bfloat16)


def body(queries, keys, values, q_gain, k_gain):
    q_normed = normalize(queries, q_gain)
    k_normed = normalize(keys, k_gain)
    q_local, k_local, v_local = (
        lax.all_to_all(q_normed, "head", split_axis=1, concat_axis=0, tiled=True),
        lax.all_to_all(k_normed, "head", split_axis=1, concat_axis=0, tiled=True),
        lax.all_to_all(values, "head", split_axis=1, concat_axis=0, tiled=True),
    )
    query_count = q_local.shape[0]
    local_heads = q_local.shape[1] // HD
    factor = 1.0 / math.sqrt(HD)
    q_heads = q_local.reshape(query_count, local_heads, HD).transpose(1, 0, 2)
    initial = (
        jnp.full((local_heads, query_count), -1e30, jnp.float32),
        jnp.zeros((local_heads, query_count), jnp.float32),
        jnp.zeros((local_heads, query_count, HD), jnp.float32),
    )
    half_rows = q_local.shape[0]
    key_piece = lax.all_gather(k_local, ("seq", "sub"), axis=0, tiled=True)
    value_piece = lax.all_gather(v_local, ("seq", "sub"), axis=0, tiled=True)
    row_count = key_piece.shape[0]
    block_size = math.gcd(row_count, 512)
    turn_count = row_count // block_size
    key_blocks = key_piece.reshape(turn_count, block_size, local_heads, HD)
    value_blocks = value_piece.reshape(turn_count, block_size, local_heads, HD)

    def advance(state, block_pair):
        key_block, value_block = block_pair
        highest, weight_sum, weighted = state
        scores = (
            jnp.einsum("hqd,khd->hqk", q_heads, key_block, preferred_element_type=jnp.float32)
            * factor
        )
        new_high = jnp.maximum(highest, jnp.max(scores, axis=-1))
        shrink = jnp.exp(highest - new_high)
        weights = jnp.exp(scores - new_high[..., None])
        new_sum = weight_sum * shrink + jnp.sum(weights, axis=-1)
        probs = weights.astype(jnp.bfloat16)
        added = jnp.einsum("hqk,khd->hqd", probs, value_block, preferred_element_type=jnp.float32)
        return ((new_high, new_sum, weighted * shrink[..., None] + added), None)

    partial_value = lax.scan(advance, initial, (key_blocks, value_blocks))[0]
    weight_sum = partial_value[1]
    weighted = partial_value[2]
    result = weighted / weight_sum[..., None]
    outputs = result.transpose(1, 0, 2).reshape(half_rows, local_heads * HD).astype(jnp.bfloat16)
    return lax.all_to_all(outputs, "head", split_axis=0, concat_axis=1, tiled=True)


MESH = pl.DeviceIdType.MESH
CHUNK = 2
AHEAD = 2


def spans_of(count):
    return [(first, min(CHUNK, count - first)) for first in range(0, count, CHUNK)]


def kernel(sizes, rows, heads, q_hbm, k_hbm, v_hbm, qg_ref, kg_ref, out_ref, q_raw, k_raw, *rest):
    nz, nx, nc = sizes
    depth = nz // 2
    groups = depth * nx * nc
    count = heads // groups
    width = count * HD
    spans = spans_of(count)
    steps = len(spans)
    own, every, o_own, o_all = (rest[i * steps:(i + 1) * steps] for i in range(4))
    load_sem, stage_sem, local_sem, send_sem, recv_sem, o_send, o_recv, o_store = rest[4 * steps:]
    z, x, c = lax.axis_index("seq"), lax.axis_index("head"), lax.axis_index("sub")
    half, place = z // depth, z % depth
    mine = (place * nx + x) * nc + c

    def peer(dh, dp, dx, dc):
        tp, tx, tc = lax.rem(place + dp, depth), lax.rem(x + dx, nx), lax.rem(c + dc, nc)
        tz = lax.rem(half + dh, 2) * depth + tp
        return {"seq": tz, "head": tx, "sub": tc}, (tp * nx + tx) * nc + tc

    def back(dp, dx, dc):
        return peer(0, (depth - dp) % depth, (nx - dx) % nx, (nc - dc) % nc)[0]

    near = [(0, dp, dx, dc) for dp in range(depth) for dx in range(nx) for dc in range(nc)]
    far = [(1, dp, dx, dc) for dp in range(depth) for dx in range(nx) for dc in range(nc)]
    offsets = near + far

    loads = [
        pltpu.make_async_copy(q_hbm, q_raw, load_sem.at[0]),
        pltpu.make_async_copy(k_hbm, k_raw, load_sem.at[1]),
    ]
    for load in loads:
        load.start()

    barrier = pltpu.get_barrier_semaphore()
    for r in offsets[1:]:
        pl.semaphore_signal(barrier, inc=1, device_id=peer(*r)[0], device_id_type=MESH)

    stages = []
    for n, (first, held) in enumerate(spans):
        for group in range(groups):
            start = group * width + first * HD
            stages.append(pltpu.make_async_copy(
                v_hbm.at[:, start:start + held * HD], own[n].at[group, 1],
                stage_sem.at[n, group]))
            stages[-1].start()

    def norm(raw, gain, which):
        total = jnp.zeros((rows, HD), jnp.float32)
        for h in range(heads):
            block = raw[:, h * HD:(h + 1) * HD].astype(jnp.float32)
            total += block * block
        mean = jnp.sum(total, axis=-1, keepdims=True) / (heads * HD)
        inverse = lax.rsqrt(mean + EPS)
        for h in range(heads):
            block = raw[:, h * HD:(h + 1) * HD].astype(jnp.float32)
            n, j = h % count // CHUNK, h % count % CHUNK
            own[n][h // count, which, :, j * HD:(j + 1) * HD] = (
                block * inverse * gain[h:h + 1, :]
            ).astype(jnp.bfloat16)

    loads[1].wait()
    norm(k_raw, kg_ref, 0)
    loads[0].wait()
    norm(q_raw, qg_ref, 2)
    for stage in stages:
        stage.wait()
    pl.semaphore_wait(barrier, len(offsets) - 1)

    def copies_of(n):
        found = []
        for r in near[1:] + far:
            i = offsets.index(r)
            device, group = peer(*r)
            source, target = own[n].at[group], every[n].at[i]
            if r[0]:
                source, target = own[n].at[group, 0:2], every[n].at[i, 0:2]
            found.append(pltpu.make_async_remote_copy(
                source, target, send_sem.at[n, i], recv_sem.at[n, i],
                device_id=device, device_id_type=MESH))
        return found

    copies = [copies_of(n) for n in range(steps)]
    locals_ = [
        pltpu.make_async_copy(own[n].at[mine], every[n].at[0], local_sem.at[n])
        for n in range(steps)
    ]

    def send(n):
        if n < steps:
            for copy in copies[n]:
                copy.start()
            locals_[n].start()

    for n in range(AHEAD):
        send(n)

    factor = 1.0 / math.sqrt(HD)

    def stacked(ref, slots, which, j):
        block = ref[0:slots, which, :, j * HD:(j + 1) * HD].astype(jnp.float32)
        return block.reshape(slots * rows, HD).astype(jnp.bfloat16)

    def attend(n, j):
        k, v = stacked(every[n], 2 * groups, 0, j), stacked(every[n], 2 * groups, 1, j)
        q = stacked(every[n], groups, 2, j)
        scores = lax.dot_general(
            q, k, (((1,), (1,)), ((), ())), preferred_element_type=jnp.float32) * factor
        weights = jnp.exp(scores - jnp.max(scores, axis=-1, keepdims=True))
        weight_sum = jnp.sum(weights, axis=-1, keepdims=True)
        weighted = jnp.dot(weights.astype(jnp.bfloat16), v, preferred_element_type=jnp.float32)
        result = (weighted / weight_sum).reshape(groups, rows, HD).astype(jnp.bfloat16)
        o_own[n][:, :, j * HD:(j + 1) * HD] = result

    def out_columns(n, group):
        first, held = spans[n]
        return out_ref.at[:, pl.ds(pl.multiple_of(group * width + first * HD, HD), held * HD)]

    o_copies, stores = [], []
    for n, (first, held) in enumerate(spans):
        locals_[n].wait()
        for copy in copies[n]:
            copy.wait_recv()
        for j in range(held):
            attend(n, j)
        for i, r in enumerate(near):
            if i:
                copy = pltpu.make_async_remote_copy(
                    o_own[n].at[i], o_all[n].at[i], o_send.at[n, i], o_recv.at[n, i],
                    device_id=back(*r[1:]), device_id_type=MESH)
                o_copies.append((n, i, r, copy))
            else:
                copy = pltpu.make_async_copy(
                    o_own[n].at[i], out_columns(n, mine), o_store.at[n, i])
                stores.append(copy)
            copy.start()
        send(n + AHEAD)
    for n, i, r, copy in o_copies:
        copy.wait_recv()
        store = pltpu.make_async_copy(
            o_all[n].at[i], out_columns(n, peer(*r)[1]), o_store.at[n, i])
        store.start()
        stores.append(store)
    for some in copies:
        for copy in some:
            copy.wait_send()
    for _, _, _, copy in o_copies:
        copy.wait_send()
    for copy in stores:
        copy.wait()


def fused(sizes, queries, keys, values, q_gain, k_gain):
    rows, total_width = queries.shape
    heads = total_width // HD
    nz, nx, nc = sizes
    groups = nz // 2 * nx * nc
    spans = spans_of(heads // groups)
    steps = len(spans)
    dma = pltpu.SemaphoreType.DMA
    half = jnp.bfloat16
    return pl.pallas_call(
        functools.partial(kernel, sizes, rows, heads),
        out_shape=jax.ShapeDtypeStruct((rows, total_width), half),
        in_specs=[pl.BlockSpec(memory_space=pl.ANY)] * 3
        + [pl.BlockSpec(memory_space=pltpu.VMEM)] * 2,
        out_specs=pl.BlockSpec(memory_space=pl.ANY),
        scratch_shapes=[
            pltpu.VMEM((rows, total_width), half),
            pltpu.VMEM((rows, total_width), half),
            *[pltpu.VMEM((groups, 3, rows, held * HD), half) for _, held in spans],
            *[pltpu.VMEM((2 * groups, 3, rows, held * HD), half) for _, held in spans],
            *[pltpu.VMEM((groups, rows, held * HD), half) for _, held in spans],
            *[pltpu.VMEM((groups, rows, held * HD), half) for _, held in spans],
            dma((2,)),
            dma((steps, groups)),
            dma((steps,)),
            dma((steps, 2 * groups)),
            dma((steps, 2 * groups)),
            dma((steps, groups)),
            dma((steps, groups)),
            dma((steps, groups)),
        ],
        compiler_params=pltpu.CompilerParams(collective_id=0, has_side_effects=True),
    )(queries, keys, values, q_gain.reshape(heads, HD), k_gain.reshape(heads, HD))


def solution(mesh):
    spec = P(("grp", "seq", "head", "sub"), None)
    sizes = (mesh.shape["seq"], mesh.shape["head"], mesh.shape["sub"])

    def run(queries, keys, values, q_gain, k_gain):
        heads = queries.shape[1] // HD
        groups = sizes[0] // 2 * sizes[1] * sizes[2]
        fits = sizes[0] % 2 == 0 and groups <= 16 and heads % groups == 0
        if fits and queries.shape[0] % 8 == 0:
            return fused(sizes, queries, keys, values, q_gain, k_gain)
        return body(queries, keys, values, q_gain, k_gain)

    return jax.shard_map(
        run, mesh=mesh, in_specs=(spec, spec, spec, P(), P()), out_specs=spec, check_vma=False)
```

```python
import functools
import math

import jax
import jax.numpy as jnp
from jax import lax
from jax.experimental import pallas as pl
from jax.experimental.pallas import tpu as pltpu
from jax.sharding import PartitionSpec as P

HD = 128


EPS = 1e-06


def normalize(matrix, gain):
    widened = matrix.astype(jnp.float32)
    inverse = lax.rsqrt(jnp.mean(widened * widened, axis=-1, keepdims=True) + EPS)
    return (widened * inverse * gain).astype(jnp.bfloat16)


def body(queries, keys, values, q_gain, k_gain):
    q_normed = normalize(queries, q_gain)
    k_normed = normalize(keys, k_gain)
    q_local, k_local, v_local = (
        lax.all_to_all(q_normed, "head", split_axis=1, concat_axis=0, tiled=True),
        lax.all_to_all(k_normed, "head", split_axis=1, concat_axis=0, tiled=True),
        lax.all_to_all(values, "head", split_axis=1, concat_axis=0, tiled=True),
    )
    query_count = q_local.shape[0]
    local_heads = q_local.shape[1] // HD
    factor = 1.0 / math.sqrt(HD)
    q_heads = q_local.reshape(query_count, local_heads, HD).transpose(1, 0, 2)
    initial = (
        jnp.full((local_heads, query_count), -1e30, jnp.float32),
        jnp.zeros((local_heads, query_count), jnp.float32),
        jnp.zeros((local_heads, query_count, HD), jnp.float32),
    )
    half_rows = q_local.shape[0]
    key_piece = lax.all_gather(k_local, ("seq", "sub"), axis=0, tiled=True)
    value_piece = lax.all_gather(v_local, ("seq", "sub"), axis=0, tiled=True)
    row_count = key_piece.shape[0]
    block_size = math.gcd(row_count, 512)
    turn_count = row_count // block_size
    key_blocks = key_piece.reshape(turn_count, block_size, local_heads, HD)
    value_blocks = value_piece.reshape(turn_count, block_size, local_heads, HD)

    def advance(state, block_pair):
        key_block, value_block = block_pair
        highest, weight_sum, weighted = state
        scores = (
            jnp.einsum("hqd,khd->hqk", q_heads, key_block, preferred_element_type=jnp.float32)
            * factor
        )
        new_high = jnp.maximum(highest, jnp.max(scores, axis=-1))
        shrink = jnp.exp(highest - new_high)
        weights = jnp.exp(scores - new_high[..., None])
        new_sum = weight_sum * shrink + jnp.sum(weights, axis=-1)
        probs = weights.astype(jnp.bfloat16)
        added = jnp.einsum("hqk,khd->hqd", probs, value_block, preferred_element_type=jnp.float32)
        return ((new_high, new_sum, weighted * shrink[..., None] + added), None)

    partial_value = lax.scan(advance, initial, (key_blocks, value_blocks))[0]
    weight_sum = partial_value[1]
    weighted = partial_value[2]
    result = weighted / weight_sum[..., None]
    outputs = result.transpose(1, 0, 2).reshape(half_rows, local_heads * HD).astype(jnp.bfloat16)
    return lax.all_to_all(outputs, "head", split_axis=0, concat_axis=1, tiled=True)


MESH = pl.DeviceIdType.MESH
SPANS = (4, 1)


def spans_of(count):
    found, first = [], 0
    for held in SPANS:
        if first < count:
            found.append((first, min(held, count - first)))
            first += held
    if first < count:
        found.append((first, count - first))
    return found


def kernel(sizes, rows, heads, q_hbm, k_hbm, v_hbm, qg_ref, kg_ref, out_ref, q_raw, k_raw, v_raw, own, every, *rest):
    nz, nx, nc = sizes
    depth = nz // 2
    groups = depth * nx * nc
    count = heads // groups
    width = count * HD
    spans = spans_of(count)
    steps = len(spans)
    o_own, o_all = rest[:steps], rest[steps:2 * steps]
    (load_sem, local_sem, near_send, near_recv, far_send, far_recv,
     o_send, o_recv, o_store) = rest[2 * steps:]
    z, x, c = lax.axis_index("seq"), lax.axis_index("head"), lax.axis_index("sub")
    half, place = z // depth, z % depth
    mine = (place * nx + x) * nc + c

    def peer(dh, dp, dx, dc):
        tp, tx, tc = lax.rem(place + dp, depth), lax.rem(x + dx, nx), lax.rem(c + dc, nc)
        tz = lax.rem(half + dh, 2) * depth + tp
        return {"seq": tz, "head": tx, "sub": tc}, (tp * nx + tx) * nc + tc

    def back(dp, dx, dc):
        return peer(0, (depth - dp) % depth, (nx - dx) % nx, (nc - dc) % nc)[0]

    near = [(0, dp, dx, dc) for dp in range(depth) for dx in range(nx) for dc in range(nc)]
    far = [(1, dp, dx, dc) for dp in range(depth) for dx in range(nx) for dc in range(nc)]
    offsets = near + far

    loads = [
        pltpu.make_async_copy(q_hbm, q_raw, load_sem.at[0]),
        pltpu.make_async_copy(k_hbm, k_raw, load_sem.at[1]),
        pltpu.make_async_copy(v_hbm, v_raw, load_sem.at[2]),
    ]
    for load in loads:
        load.start()

    barrier = pltpu.get_barrier_semaphore()
    for r in offsets[1:]:
        pl.semaphore_signal(barrier, inc=1, device_id=peer(*r)[0], device_id_type=MESH)

    def norm(raw, gain, place_of):
        total = jnp.zeros((rows, HD), jnp.float32)
        for h in range(heads):
            block = raw[:, h * HD:(h + 1) * HD].astype(jnp.float32)
            total += block * block
        mean = jnp.sum(total, axis=-1, keepdims=True) / (heads * HD)
        inverse = lax.rsqrt(mean + EPS)
        for h in range(heads):
            block = raw[:, h * HD:(h + 1) * HD].astype(jnp.float32)
            own[h // count, place_of(h % count)] = (
                block * inverse * gain[h:h + 1, :]
            ).astype(jnp.bfloat16)

    loads[1].wait()
    norm(k_raw, kg_ref, lambda j: 2 * j)
    loads[0].wait()
    norm(q_raw, qg_ref, lambda j: 2 * count + j)
    loads[2].wait()
    for h in range(heads):
        own[h // count, 2 * (h % count) + 1] = v_raw[:, h * HD:(h + 1) * HD]
    pl.semaphore_wait(barrier, len(offsets) - 1)

    near_copies, far_copies = [], [[] for _ in spans]
    for i, r in enumerate(offsets):
        device, group = peer(*r)
        if r[0]:
            for n, (first, held) in enumerate(spans):
                part = slice(2 * first, 2 * (first + held))
                far_copies[n].append(pltpu.make_async_remote_copy(
                    own.at[group, part], every.at[i, part],
                    far_send.at[n, i - groups], far_recv.at[n, i - groups],
                    device_id=device, device_id_type=MESH))
        elif i:
            near_copies.append(pltpu.make_async_remote_copy(
                own.at[group], every.at[i], near_send.at[i], near_recv.at[i],
                device_id=device, device_id_type=MESH))
    for copy in near_copies:
        copy.start()
    for some in far_copies:
        for copy in some:
            copy.start()
    local = pltpu.make_async_copy(own.at[mine], every.at[0], local_sem)
    local.start()
    local.wait()

    factor = 1.0 / math.sqrt(HD)

    def stacked(slots, index):
        block = every[0:slots, index].astype(jnp.float32)
        return block.reshape(slots * rows, HD).astype(jnp.bfloat16)

    def attend(n, first, j):
        k, v = stacked(2 * groups, 2 * (first + j)), stacked(2 * groups, 2 * (first + j) + 1)
        q = stacked(groups, 2 * count + first + j)
        scores = lax.dot_general(
            q, k, (((1,), (1,)), ((), ())), preferred_element_type=jnp.float32) * factor
        weights = jnp.exp(scores - jnp.max(scores, axis=-1, keepdims=True))
        weight_sum = jnp.sum(weights, axis=-1, keepdims=True)
        weighted = jnp.dot(weights.astype(jnp.bfloat16), v, preferred_element_type=jnp.float32)
        result = (weighted / weight_sum).reshape(groups, rows, HD).astype(jnp.bfloat16)
        o_own[n][:, :, j * HD:(j + 1) * HD] = result

    def out_columns(n, group):
        first, held = spans[n]
        return out_ref.at[:, pl.ds(pl.multiple_of(group * width + first * HD, HD), held * HD)]

    o_copies, stores = [], []
    for n, (first, held) in enumerate(spans):
        if n == 0:
            for copy in near_copies:
                copy.wait_recv()
        for copy in far_copies[n]:
            copy.wait_recv()
        for j in range(held):
            attend(n, first, j)
        for i, r in enumerate(near):
            if i:
                copy = pltpu.make_async_remote_copy(
                    o_own[n].at[i], o_all[n].at[i], o_send.at[n, i], o_recv.at[n, i],
                    device_id=back(*r[1:]), device_id_type=MESH)
                o_copies.append((n, i, r, copy))
            else:
                copy = pltpu.make_async_copy(
                    o_own[n].at[i], out_columns(n, mine), o_store.at[n, i])
                stores.append(copy)
            copy.start()
    for n, i, r, copy in o_copies:
        copy.wait_recv()
        store = pltpu.make_async_copy(
            o_all[n].at[i], out_columns(n, peer(*r)[1]), o_store.at[n, i])
        store.start()
        stores.append(store)
    for some in [near_copies] + far_copies:
        for copy in some:
            copy.wait_send()
    for _, _, _, copy in o_copies:
        copy.wait_send()
    for copy in stores:
        copy.wait()


def fused(sizes, queries, keys, values, q_gain, k_gain):
    rows, total_width = queries.shape
    heads = total_width // HD
    nz, nx, nc = sizes
    groups = nz // 2 * nx * nc
    count = heads // groups
    spans = spans_of(count)
    steps = len(spans)
    dma = pltpu.SemaphoreType.DMA
    half = jnp.bfloat16
    return pl.pallas_call(
        functools.partial(kernel, sizes, rows, heads),
        out_shape=jax.ShapeDtypeStruct((rows, total_width), half),
        in_specs=[pl.BlockSpec(memory_space=pl.ANY)] * 3
        + [pl.BlockSpec(memory_space=pltpu.VMEM)] * 2,
        out_specs=pl.BlockSpec(memory_space=pl.ANY),
        scratch_shapes=[
            pltpu.VMEM((rows, total_width), half),
            pltpu.VMEM((rows, total_width), half),
            pltpu.VMEM((rows, total_width), half),
            pltpu.VMEM((groups, 3 * count, rows, HD), half),
            pltpu.VMEM((2 * groups, 3 * count, rows, HD), half),
            *[pltpu.VMEM((groups, rows, held * HD), half) for _, held in spans],
            *[pltpu.VMEM((groups, rows, held * HD), half) for _, held in spans],
            dma((3,)),
            dma(()),
            dma((groups,)),
            dma((groups,)),
            dma((steps, groups)),
            dma((steps, groups)),
            dma((steps, groups)),
            dma((steps, groups)),
            dma((steps, groups)),
        ],
        compiler_params=pltpu.CompilerParams(collective_id=0, has_side_effects=True),
    )(queries, keys, values, q_gain.reshape(heads, HD), k_gain.reshape(heads, HD))


def solution(mesh):
    spec = P(("grp", "seq", "head", "sub"), None)
    sizes = (mesh.shape["seq"], mesh.shape["head"], mesh.shape["sub"])

    def run(queries, keys, values, q_gain, k_gain):
        heads = queries.shape[1] // HD
        groups = sizes[0] // 2 * sizes[1] * sizes[2]
        fits = sizes[0] % 2 == 0 and groups <= 16 and heads % groups == 0
        if fits and queries.shape[0] % 8 == 0:
            return fused(sizes, queries, keys, values, q_gain, k_gain)
        return body(queries, keys, values, q_gain, k_gain)

    return jax.shard_map(
        run, mesh=mesh, in_specs=(spec, spec, spec, P(), P()), out_specs=spec, check_vma=False)
```

```python
import functools
import math

import jax
import jax.numpy as jnp
from jax import lax
from jax.experimental import pallas as pl
from jax.experimental.pallas import tpu as pltpu
from jax.sharding import PartitionSpec as P

HD = 128


EPS = 1e-06


def normalize(matrix, gain):
    widened = matrix.astype(jnp.float32)
    inverse = lax.rsqrt(jnp.mean(widened * widened, axis=-1, keepdims=True) + EPS)
    return (widened * inverse * gain).astype(jnp.bfloat16)


def body(queries, keys, values, q_gain, k_gain):
    q_normed = normalize(queries, q_gain)
    k_normed = normalize(keys, k_gain)
    q_local, k_local, v_local = (
        lax.all_to_all(q_normed, "head", split_axis=1, concat_axis=0, tiled=True),
        lax.all_to_all(k_normed, "head", split_axis=1, concat_axis=0, tiled=True),
        lax.all_to_all(values, "head", split_axis=1, concat_axis=0, tiled=True),
    )
    query_count = q_local.shape[0]
    local_heads = q_local.shape[1] // HD
    factor = 1.0 / math.sqrt(HD)
    q_heads = q_local.reshape(query_count, local_heads, HD).transpose(1, 0, 2)
    initial = (
        jnp.full((local_heads, query_count), -1e30, jnp.float32),
        jnp.zeros((local_heads, query_count), jnp.float32),
        jnp.zeros((local_heads, query_count, HD), jnp.float32),
    )
    half_rows = q_local.shape[0]
    key_piece = lax.all_gather(k_local, ("seq", "sub"), axis=0, tiled=True)
    value_piece = lax.all_gather(v_local, ("seq", "sub"), axis=0, tiled=True)
    row_count = key_piece.shape[0]
    block_size = math.gcd(row_count, 512)
    turn_count = row_count // block_size
    key_blocks = key_piece.reshape(turn_count, block_size, local_heads, HD)
    value_blocks = value_piece.reshape(turn_count, block_size, local_heads, HD)

    def advance(state, block_pair):
        key_block, value_block = block_pair
        highest, weight_sum, weighted = state
        scores = (
            jnp.einsum("hqd,khd->hqk", q_heads, key_block, preferred_element_type=jnp.float32)
            * factor
        )
        new_high = jnp.maximum(highest, jnp.max(scores, axis=-1))
        shrink = jnp.exp(highest - new_high)
        weights = jnp.exp(scores - new_high[..., None])
        new_sum = weight_sum * shrink + jnp.sum(weights, axis=-1)
        probs = weights.astype(jnp.bfloat16)
        added = jnp.einsum("hqk,khd->hqd", probs, value_block, preferred_element_type=jnp.float32)
        return ((new_high, new_sum, weighted * shrink[..., None] + added), None)

    partial_value = lax.scan(advance, initial, (key_blocks, value_blocks))[0]
    weight_sum = partial_value[1]
    weighted = partial_value[2]
    result = weighted / weight_sum[..., None]
    outputs = result.transpose(1, 0, 2).reshape(half_rows, local_heads * HD).astype(jnp.bfloat16)
    return lax.all_to_all(outputs, "head", split_axis=0, concat_axis=1, tiled=True)


MESH = pl.DeviceIdType.MESH
SPANS = (4, 1)


def spans_of(count):
    found, first = [], 0
    for held in SPANS:
        if first < count:
            found.append((first, min(held, count - first)))
            first += held
    if first < count:
        found.append((first, count - first))
    return found


def kernel(sizes, rows, heads, q_hbm, k_hbm, v_hbm, qg_ref, kg_ref, out_ref, q_raw, k_raw, v_raw, own, every, *rest):
    nz, nx, nc = sizes
    depth = nz // 2
    groups = depth * nx * nc
    count = heads // groups
    width = count * HD
    spans = spans_of(count)
    steps = len(spans)
    o_own, o_all = rest[:steps], rest[steps:2 * steps]
    (load_sem, local_sem, near_send, near_recv, far_send, far_recv,
     o_send, o_recv, o_store) = rest[2 * steps:]
    z, x, c = lax.axis_index("seq"), lax.axis_index("head"), lax.axis_index("sub")
    half, place = z // depth, z % depth
    mine = (place * nx + x) * nc + c

    def peer(dh, dp, dx, dc):
        tp, tx, tc = lax.rem(place + dp, depth), lax.rem(x + dx, nx), lax.rem(c + dc, nc)
        tz = lax.rem(half + dh, 2) * depth + tp
        return {"seq": tz, "head": tx, "sub": tc}, (tp * nx + tx) * nc + tc

    def back(dp, dx, dc):
        return peer(0, (depth - dp) % depth, (nx - dx) % nx, (nc - dc) % nc)[0]

    near = [(0, dp, dx, dc) for dp in range(depth) for dx in range(nx) for dc in range(nc)]
    far = [(1, dp, dx, dc) for dx in range(nx) for dc in range(nc) for dp in reversed(range(depth))]
    offsets = near + far

    loads = [
        pltpu.make_async_copy(q_hbm, q_raw, load_sem.at[0]),
        pltpu.make_async_copy(k_hbm, k_raw, load_sem.at[1]),
        pltpu.make_async_copy(v_hbm, v_raw, load_sem.at[2]),
    ]
    for load in loads:
        load.start()

    barrier = pltpu.get_barrier_semaphore()
    for r in offsets[1:]:
        pl.semaphore_signal(barrier, inc=1, device_id=peer(*r)[0], device_id_type=MESH)

    def norm(raw, gain, place_of):
        total = jnp.zeros((rows, HD), jnp.float32)
        for h in range(heads):
            block = raw[:, h * HD:(h + 1) * HD].astype(jnp.float32)
            total += block * block
        mean = jnp.sum(total, axis=-1, keepdims=True) / (heads * HD)
        inverse = lax.rsqrt(mean + EPS)
        for h in range(heads):
            block = raw[:, h * HD:(h + 1) * HD].astype(jnp.float32)
            own[h // count, place_of(h % count)] = (
                block * inverse * gain[h:h + 1, :]
            ).astype(jnp.bfloat16)

    loads[1].wait()
    norm(k_raw, kg_ref, lambda j: 2 * j)
    loads[0].wait()
    norm(q_raw, qg_ref, lambda j: 2 * count + j)
    loads[2].wait()
    for h in range(heads):
        own[h // count, 2 * (h % count) + 1] = v_raw[:, h * HD:(h + 1) * HD]
    pl.semaphore_wait(barrier, len(offsets) - 1)

    near_copies, far_copies = [], [[] for _ in spans]
    for i, r in enumerate(offsets):
        device, group = peer(*r)
        if r[0]:
            for n, (first, held) in enumerate(spans):
                part = slice(2 * first, 2 * (first + held))
                far_copies[n].append(pltpu.make_async_remote_copy(
                    own.at[group, part], every.at[i, part],
                    far_send.at[n, i - groups], far_recv.at[n, i - groups],
                    device_id=device, device_id_type=MESH))
        elif i:
            near_copies.append(pltpu.make_async_remote_copy(
                own.at[group], every.at[i], near_send.at[i], near_recv.at[i],
                device_id=device, device_id_type=MESH))
    for copy in near_copies:
        copy.start()
    for some in far_copies:
        for copy in some:
            copy.start()
    local = pltpu.make_async_copy(own.at[mine], every.at[0], local_sem)
    local.start()
    local.wait()

    factor = 1.0 / math.sqrt(HD)

    def stacked(slots, index):
        block = every[0:slots, index].astype(jnp.float32)
        return block.reshape(slots * rows, HD).astype(jnp.bfloat16)

    def attend(n, first, j):
        k, v = stacked(2 * groups, 2 * (first + j)), stacked(2 * groups, 2 * (first + j) + 1)
        q = stacked(groups, 2 * count + first + j)
        scores = lax.dot_general(
            q, k, (((1,), (1,)), ((), ())), preferred_element_type=jnp.float32) * factor
        weights = jnp.exp(scores - jnp.max(scores, axis=-1, keepdims=True))
        weight_sum = jnp.sum(weights, axis=-1, keepdims=True)
        weighted = jnp.dot(weights.astype(jnp.bfloat16), v, preferred_element_type=jnp.float32)
        result = (weighted / weight_sum).reshape(groups, rows, HD).astype(jnp.bfloat16)
        o_own[n][:, :, j * HD:(j + 1) * HD] = result

    def out_columns(n, group):
        first, held = spans[n]
        return out_ref.at[:, pl.ds(pl.multiple_of(group * width + first * HD, HD), held * HD)]

    o_copies, stores = [], []
    for n, (first, held) in enumerate(spans):
        if n == 0:
            for copy in near_copies:
                copy.wait_recv()
        for copy in far_copies[n]:
            copy.wait_recv()
        for j in range(held):
            attend(n, first, j)
        for i, r in enumerate(near):
            if i:
                copy = pltpu.make_async_remote_copy(
                    o_own[n].at[i], out_columns(n, mine), o_send.at[n, i], o_recv.at[n, i],
                    device_id=back(*r[1:]), device_id_type=MESH)
                o_copies.append((n, i, r, copy))
            else:
                copy = pltpu.make_async_copy(
                    o_own[n].at[i], out_columns(n, mine), o_store.at[n, i])
                stores.append(copy)
            copy.start()
    for n, i, r, copy in o_copies:
        copy.wait_recv()
    for some in [near_copies] + far_copies:
        for copy in some:
            copy.wait_send()
    for _, _, _, copy in o_copies:
        copy.wait_send()
    for copy in stores:
        copy.wait()


def fused(sizes, queries, keys, values, q_gain, k_gain):
    rows, total_width = queries.shape
    heads = total_width // HD
    nz, nx, nc = sizes
    groups = nz // 2 * nx * nc
    count = heads // groups
    spans = spans_of(count)
    steps = len(spans)
    dma = pltpu.SemaphoreType.DMA
    half = jnp.bfloat16
    return pl.pallas_call(
        functools.partial(kernel, sizes, rows, heads),
        out_shape=jax.ShapeDtypeStruct((rows, total_width), half),
        in_specs=[pl.BlockSpec(memory_space=pl.ANY)] * 3
        + [pl.BlockSpec(memory_space=pltpu.VMEM)] * 2,
        out_specs=pl.BlockSpec(memory_space=pl.ANY),
        scratch_shapes=[
            pltpu.VMEM((rows, total_width), half),
            pltpu.VMEM((rows, total_width), half),
            pltpu.VMEM((rows, total_width), half),
            pltpu.VMEM((groups, 3 * count, rows, HD), half),
            pltpu.VMEM((2 * groups, 3 * count, rows, HD), half),
            *[pltpu.VMEM((groups, rows, held * HD), half) for _, held in spans],
            *[pltpu.VMEM((groups, rows, held * HD), half) for _, held in spans],
            dma((3,)),
            dma(()),
            dma((groups,)),
            dma((groups,)),
            dma((steps, groups)),
            dma((steps, groups)),
            dma((steps, groups)),
            dma((steps, groups)),
            dma((steps, groups)),
        ],
        compiler_params=pltpu.CompilerParams(collective_id=0, has_side_effects=True),
    )(queries, keys, values, q_gain.reshape(heads, HD), k_gain.reshape(heads, HD))


def solution(mesh):
    spec = P(("grp", "seq", "head", "sub"), None)
    sizes = (mesh.shape["seq"], mesh.shape["head"], mesh.shape["sub"])

    def run(queries, keys, values, q_gain, k_gain):
        heads = queries.shape[1] // HD
        groups = sizes[0] // 2 * sizes[1] * sizes[2]
        fits = sizes[0] % 2 == 0 and groups <= 16 and heads % groups == 0
        if fits and queries.shape[0] % 8 == 0:
            return fused(sizes, queries, keys, values, q_gain, k_gain)
        return body(queries, keys, values, q_gain, k_gain)

    return jax.shard_map(
        run, mesh=mesh, in_specs=(spec, spec, spec, P(), P()), out_specs=spec, check_vma=False)
```
